32 devices in a mesh: band: 4 (over y, x), lon: 8 (over z, core).
Axes of the slice: x: 2, y: 2, z: 4, core: 2. Of those that a mesh axis runs over, the one named last changes fastest.
Arguments:
- atm_state: bfloat16 [2048, 64, 128], P(('band', 'lon')), may hold values from -6 to 6
- ocean_state: bfloat16 [4096, 64, 128], P(('band', 'lon')), may hold values from -6 to 6
- wet_mask: int32 [4096, 128], P(('band', 'lon')), may hold values 0 or 1
- remap_tiles: bfloat16 [32, 128, 128], replicated, may hold values from -0.5 to 0.5
- intersection_atm: int32 [32, 32, 2], P(('band', 'lon')), may hold values from 0 to 63
- intersection_ocean: int32 [32, 32, 2], P(('band', 'lon')), may hold values from 0 to 127
- intersection_tile: int32 [32, 32, 2], P(('band', 'lon')), may hold values from 0 to 31
- peer_count: int32 [32, 32], P(('band', 'lon')), may hold values from 0 to 2, as said below
- w_in: bfloat16 [256, 128], replicated, may hold values from -0.5 to 0.5
- w_mid: bfloat16 [2, 256, 256], replicated, may hold values from -0.375 to 0.375
- b_hidden: float32 [3, 256], replicated, may hold values from -3 to 3
- w_out: bfloat16 [16, 256], replicated, may hold values from -0.375 to 0.375
- b_out: float32 [16], replicated, may hold values from -3 to 3
- up_atm: float32 [64, 16], replicated, may hold values from -1.5 to 1.5
- up_ocean: float32 [64, 16], replicated, may hold values from -1.5 to 1.5
Outputs:
- atm_flux: float32 [2048, 16, 128], P(('band', 'lon'))
- ocean_flux: float32 [4096, 16, 128], P(('band', 'lon'))
The draws below stay inside these ranges and needn't reach their ends.
Inputs may be any that keep to these rules, and one draw needn't show every extreme that they name: `peer_count`: A slot is live when its index is below the count. In every draw one owner receives 2 live slots from every device; a few devices have live slots to nearly every owner, the others to about a quarter.
All inputs are finite; a program needn't handle non-finite values. No bound on the sum of `wet_mask` on one device may be relied on, other than what follows from the above.
Results may differ from the reference program's by a relative error of at most 0.008.
Values may be sent and summed in bfloat16 or wider, within the bound.
A program may use at most 128 MiB of HBM per device.

```python
import jax
import jax.numpy as jnp
from jax import lax

C = 64
CO = 64
CF = 16
HID = 256
BA = 128
BO = 128
NTILE = 32
PEER_CAP = 2
ABLK_DEV = 64
OBLK_DEV = 128
PEERS = 32
NAB = 2048
NOB = 4096


def draw_peer_count(key, part):
    keys = jax.random.split(jax.random.fold_in(key, 11), 4)
    heavy = jax.random.randint(keys[0], (PEERS, 1), 0, 8) == 0
    threshold = jnp.where(heavy, 90, 25)
    chance = jax.random.randint(keys[1], (PEERS, PEERS), 0, 100)
    amount = jax.random.randint(keys[2], (PEERS, PEERS), 1, PEER_CAP + 1)
    counts = jnp.where(chance < threshold, amount, 0)
    full_owner = jax.random.randint(keys[3], (), 0, PEERS)
    column = jnp.arange(PEERS, dtype=jnp.int32)[None, :] == full_owner
    counts = jnp.where(column, PEER_CAP, counts)
    return counts.astype(jnp.int32)


def touch_ends(array, key, least, high):
    shape = array.shape
    place = [jax.random.randint(jax.random.fold_in(key, axis), (), 0, shape[axis]) for axis in range(len(shape))]
    array = array.at[tuple(place)].set(least)
    longest = shape.index(max(shape))
    place[longest] = (place[longest] + 1) % shape[longest]
    return array.at[tuple(place)].set(high)


def level_of(stream_key, dims, cuts, low, largest):
    level = 1.0
    for position, parts in cuts:
        draws = jax.random.uniform(jax.random.fold_in(jax.random.fold_in(stream_key, 6), position), (parts,), jnp.float32, low / len(cuts), largest / len(cuts))
        level = level * jnp.repeat(jnp.exp(draws), dims[position] // parts).reshape((-1,) + (1,) * (len(dims) - 1 - position))
    return level


def gaussian(stream_key, dims, deviation, most, cuts=(), kind=jnp.bfloat16):
    values = deviation * jax.random.normal(stream_key, dims, jnp.float32)
    if cuts:
        values = values * level_of(stream_key, dims, cuts, -0.22, 0.18)
    return jnp.clip(values, -most, most).astype(kind)


def setup_inputs(seed: int = 0) -> dict:
    seeds = jax.random.split(jax.random.key(seed), 16)
    atm_state = gaussian(seeds[0], (NAB, C, BA), 1.0, 6.0, ((0, 32),))
    ocean_state = gaussian(seeds[1], (NOB, CO, BO), 1.0, 6.0, ((0, 32),))
    wet_mask = touch_ends((jax.random.randint(seeds[2], (NOB, BO), 0, 3) < 2).astype(jnp.int32), jax.random.fold_in(seeds[2], 1), 0, 1)
    remap_tiles = gaussian(seeds[3], (NTILE, BA, BO), BA ** -0.5, 0.5)
    intersection_atm = touch_ends(jax.random.randint(seeds[4], (PEERS, PEERS, PEER_CAP), 0, ABLK_DEV), jax.random.fold_in(seeds[4], 1), 0, ABLK_DEV - 1).astype(jnp.int32)
    intersection_ocean = touch_ends(jax.random.randint(seeds[5], (PEERS, PEERS, PEER_CAP), 0, OBLK_DEV), jax.random.fold_in(seeds[5], 1), 0, OBLK_DEV - 1).astype(jnp.int32)
    intersection_tile = touch_ends(jax.random.randint(seeds[6], (PEERS, PEERS, PEER_CAP), 0, NTILE), jax.random.fold_in(seeds[6], 1), 0, NTILE - 1).astype(jnp.int32)
    peer_count = draw_peer_count(jax.random.fold_in(seeds[15], 71), 0)
    w_in = gaussian(seeds[8], (HID, C + CO), (C + CO) ** -0.5, 0.5)
    w_mid = gaussian(seeds[9], (2, HID, HID), HID ** -0.5, 0.375)
    b_hidden = gaussian(seeds[10], (3, HID), 0.5, 3.0, (), jnp.float32)
    w_out = gaussian(seeds[11], (CF, HID), HID ** -0.5, 0.375)
    b_out = gaussian(seeds[12], (CF,), 0.5, 3.0, (), jnp.float32)
    up_atm = gaussian(seeds[13], (C, CF), CF ** -0.5, 1.5, (), jnp.float32)
    up_ocean = gaussian(seeds[14], (CO, CF), CF ** -0.5, 1.5, (), jnp.float32)
    return dict(atm_state=atm_state, ocean_state=ocean_state, wet_mask=wet_mask, remap_tiles=remap_tiles, intersection_atm=intersection_atm, intersection_ocean=intersection_ocean, intersection_tile=intersection_tile, peer_count=peer_count, w_in=w_in, w_mid=w_mid, b_hidden=b_hidden, w_out=w_out, b_out=b_out, up_atm=up_atm, up_ocean=up_ocean)


def flux_block(atm_group, ocean_group, remap, wet_rows, w_in, w_mid, b_hidden, w_out, b_out):
    remap_float = remap.astype(jnp.float32)
    on_ocean = jnp.einsum('sca,sab->scb', atm_group.astype(jnp.float32), remap_float).astype(jnp.bfloat16)
    hidden = jnp.concatenate([on_ocean, ocean_group], axis=1)
    hidden = jax.nn.silu(jnp.einsum('hk,skb->shb', w_in.astype(jnp.float32), hidden.astype(jnp.float32)) + b_hidden[0][None, :, None]).astype(jnp.bfloat16)
    for level_index in range(w_mid.shape[0]):
        hidden = jax.nn.silu(jnp.einsum('hk,skb->shb', w_mid[level_index].astype(jnp.float32), hidden.astype(jnp.float32)) + b_hidden[level_index + 1][None, :, None]).astype(jnp.bfloat16)
    fluxes = ((jnp.einsum('fh,shb->sfb', w_out.astype(jnp.float32), hidden.astype(jnp.float32)) + b_out[None, :, None]) * wet_rows[:, None, :]).astype(jnp.bfloat16)
    back = jnp.einsum('sfb,sab->sfa', fluxes.astype(jnp.float32), remap_float)
    return fluxes.astype(jnp.float32), back


def reference(atm_state, ocean_state, wet_mask, remap_tiles, intersection_atm, intersection_ocean, intersection_tile, peer_count, w_in, w_mid, b_hidden, w_out, b_out, up_atm, up_ocean):
    def coupling(atm_now, ocean_now):
        def one_device(carry, device):
            atm_total, ocean_total = carry
            owners = jnp.arange(PEERS, dtype=jnp.int32)
            atm_rows = (owners[:, None] * ABLK_DEV + intersection_atm[device]).reshape(-1).astype(jnp.int32)
            ocean_rows = (device * OBLK_DEV + intersection_ocean[device]).reshape(-1).astype(jnp.int32)
            live_mask = (jnp.arange(PEER_CAP, dtype=jnp.int32)[None, :] < peer_count[device][:, None]).reshape(-1)
            wet_rows = wet_mask[ocean_rows].astype(jnp.float32) * live_mask.astype(jnp.float32)[:, None]
            remap = remap_tiles[intersection_tile[device].reshape(-1)]
            fluxes, back = flux_block(atm_now[atm_rows], ocean_now[ocean_rows], remap, wet_rows, w_in, w_mid, b_hidden, w_out, b_out)
            return (atm_total.at[atm_rows].add(back), ocean_total.at[ocean_rows].add(fluxes)), None
        start = (jnp.zeros((NAB, CF, BA), jnp.float32), jnp.zeros((NOB, CF, BO), jnp.float32))
        totals, unused = lax.scan(one_device, start, jnp.arange(PEERS, dtype=jnp.int32))
        return totals

    atm_total, ocean_total = coupling(atm_state, ocean_state)
    atm_next = (atm_state.astype(jnp.float32) + jnp.einsum('cf,nfa->nca', up_atm, atm_total, precision=lax.Precision.HIGHEST)).astype(jnp.bfloat16)
    ocean_next = (ocean_state.astype(jnp.float32) + wet_mask.astype(jnp.float32)[:, None, :] * jnp.einsum('cf,nfb->ncb', up_ocean, ocean_total, precision=lax.Precision.HIGHEST)).astype(jnp.bfloat16)
    atm_flux, ocean_flux = coupling(atm_next, ocean_next)
    return (atm_flux, ocean_flux)
```

```python
import functools

import jax
import jax.numpy as jnp
from jax import lax
from jax.experimental import pallas as pl
from jax.experimental.pallas import tpu as pltpu
from jax.sharding import PartitionSpec as P

MESH = pl.DeviceIdType.MESH
BF = jnp.bfloat16
F32 = jnp.float32
GROUP = 4


def dot(a, b):
    return jnp.dot(a, b, preferred_element_type=F32)


def silu_half(u):
    return (u + u * jnp.tanh(u)).astype(BF)


def kernel(
    n, lon_n,
    meta, want, orows, atm, ocean, wet, remap, w_in, w_mid, b_cols, w_out, b_out, up_a, up_o,
    out_a, out_o,
    idx_send, idx_recv, idx_smem, blk_send, blk_recv,
    bk_send, bk_recv, fw_send, fw_recv, bk2_send, bk2_recv,
    hid, w_in_h, w_mid_h, fx, fo, xr, ocean_slot, m_a, a_t, m_o, g_t,
    local_sem, s_idx, r_idx, s_blk, r_blk, s_bk, r_bk, s_fw, r_fw, s_bk2, r_bk2,
):
    me = lax.axis_index("band") * lon_n + lax.axis_index("lon")
    slots = 2 * n
    cf = out_a.shape[0] // atm.shape[0]
    ablk = atm.shape[0]
    oblk = ocean.shape[0]
    cells = atm.shape[2]
    ch = atm.shape[1]

    def dev(t):
        return (t // lon_n, t % lon_n)

    def ahead(k):
        return (me + k) % n

    def behind(k):
        return (me + n - k) % n

    def copy_to(src, dst, s_sem, r_sem, q):
        return pltpu.make_async_remote_copy(
            src_ref=src.at[:, q], dst_ref=dst.at[:, me],
            send_sem=s_sem.at[q], recv_sem=r_sem.at[me],
            device_id=dev(q), device_id_type=MESH,
        )

    def arrival(src, dst, s_sem, r_sem, q):
        return pltpu.make_async_remote_copy(
            src_ref=src.at[:, q], dst_ref=dst.at[:, q],
            send_sem=s_sem.at[q], recv_sem=r_sem.at[q],
            device_id=dev(q), device_id_type=MESH,
        )

    def each(fn):
        @pl.loop(1, n)
        def _(k):
            fn(k)

    barrier = pltpu.get_barrier_semaphore()
    each(lambda k: pl.semaphore_signal(barrier, inc=1, device_id=dev(ahead(k)), device_id_type=MESH))

    lane = lax.broadcasted_iota(jnp.int32, (n, 128), 1)
    wanted = want[0]
    rows = jnp.where(lane == 0, wanted[:, 0:1], jnp.where(lane == 1, wanted[:, 1:2], 0))
    idx_send[0] = rows.reshape(n, 1, 128)
    idx_recv[0, pl.ds(me, 1)] = idx_send[0, pl.ds(me, 1)]
    pl.semaphore_wait(barrier, n - 1)

    each(lambda k: copy_to(idx_send, idx_recv, s_idx, r_idx, ahead(k)).start())

    w_in_h[...] = (w_in[...].astype(F32) * 0.5).astype(BF)
    for l in range(2):
        w_mid_h[l] = (w_mid[l].astype(F32) * 0.5).astype(BF)
    oc = orows[0]
    io = lax.broadcasted_iota(jnp.int32, (n, oblk), 1)
    g = jnp.concatenate([(oc[:, j : j + 1] == io).astype(F32) for j in range(2)], axis=0)
    g_t[...] = g.T.astype(BF)
    gb = g.astype(BF)
    m_o[...] = lax.dot_general(gb, gb, (((1,), (1,)), ((), ())), preferred_element_type=F32).astype(BF)

    each(lambda k: arrival(idx_send, idx_recv, s_idx, r_idx, behind(k)).wait_recv())
    to_smem = pltpu.make_async_copy(idx_recv, idx_smem, local_sem)
    to_smem.start()
    to_smem.wait()

    @pl.loop(1, n)
    def _(k):
        q = ahead(k)
        for j in range(2):
            blk_send[j, q] = atm[idx_smem[0, q, 0, j]]
        copy_to(blk_send, blk_recv, s_blk, r_blk, q).start()

    for j in range(2):
        blk_recv[j, me] = atm[idx_smem[0, me, 0, j]]

    got = idx_recv[0].reshape(n, 128)
    ia = lax.broadcasted_iota(jnp.int32, (n, ablk), 1)
    a = jnp.concatenate([(got[:, j : j + 1] == ia).astype(F32) for j in range(2)], axis=0)
    a_t[...] = a.T.astype(BF)
    ab = a.astype(BF)
    m_a[...] = lax.dot_general(ab, ab, (((1,), (1,)), ((), ())), preferred_element_type=F32).astype(BF)

    def network(b, second, back_send, back_recv, s_sem, r_sem):
        where = []
        for i in range(GROUP):
            k = b * GROUP + i
            q = behind(k)

            @pl.when(k > 0)
            def _():
                if second:
                    arrival(fw_send, fw_recv, s_fw, r_fw, q).wait_recv()
                else:
                    arrival(blk_send, blk_recv, s_blk, r_blk, q).wait_recv()

            for j in range(2):
                where.append((k, j, q, j * n + q))
        wet_rows = []
        for t, (k, j, q, s) in enumerate(where):
            cols = slice(t * cells, (t + 1) * cells)
            row = wet[pl.ds(meta[s], 1), :]
            wet_rows.append((row * meta[2 * slots + s]).astype(F32))
            block = blk_recv[j, q]
            sea = ocean[meta[s]]
            if second:
                fwd = fw_recv[j, q].astype(F32)
                block = (
                    block.astype(F32)
                    + jnp.dot(up_a[...], fwd, precision=lax.Precision.HIGHEST, preferred_element_type=F32)
                ).astype(BF)
                total = fo[pl.ds(pl.multiple_of(s * cf, cf), cf), :]
                sea = (
                    sea.astype(F32)
                    + row.astype(F32)
                    * jnp.dot(up_o[...], total, precision=lax.Precision.HIGHEST, preferred_element_type=F32)
                ).astype(BF)
            hid[0:ch, cols] = dot(block, remap[meta[slots + s]]).astype(BF)
            hid[ch:, cols] = sea
        h = silu_half(dot(w_in_h[...], hid[...]) + b_cols[:, 0:1])
        h = silu_half(dot(w_mid_h[0], h) + b_cols[:, 1:2])
        h = silu_half(dot(w_mid_h[1], h) + b_cols[:, 2:3])
        flux = dot(w_out[...], h) + b_out[...]
        flux = (flux * jnp.concatenate(wet_rows, axis=1)).astype(BF)
        for t, (k, j, q, s) in enumerate(where):
            one = flux[:, t * cells : (t + 1) * cells]
            fx[pl.ds(pl.multiple_of(s * cf, cf), cf), :] = one.astype(F32)
            back = lax.dot_general(
                one, remap[meta[slots + s]], (((1,), (1,)), ((), ())), preferred_element_type=F32
            )
            back_send[j, q] = back.astype(BF)
        for i in range(GROUP):
            k, j, q, s = where[2 * i]

            @pl.when(k > 0)
            def _():
                copy_to(back_send, back_recv, s_sem, r_sem, q).start()

    def collect(back_send, back_recv, s_sem, r_sem):
        for j in range(2):
            back_recv[j, me] = back_send[j, me]
        each(lambda k: arrival(back_send, back_recv, s_sem, r_sem, behind(k)).wait_recv())
        xr[...] = back_recv[...].reshape(slots * cf, cells).astype(F32)

    def gathered(matrix, src, dst, count):
        for f in range(cf):
            x = src[pl.ds(f, slots, stride=cf), :].astype(BF)
            dst[pl.ds(f, count, stride=cf), :] = dot(matrix[...], x)

    @pl.loop(0, n // GROUP)
    def _(b):
        network(b, False, bk_send, bk_recv, s_bk, r_bk)

    gathered(m_o, fx, fo, slots)
    collect(bk_send, bk_recv, s_bk, r_bk)
    gathered(m_a, xr, xr, slots)
    fw_send[...] = xr[...].reshape(2, n, cf, cells).astype(BF)
    each(lambda k: copy_to(fw_send, fw_recv, s_fw, r_fw, ahead(k)).start())
    for j in range(2):
        fw_recv[j, me] = fw_send[j, me]

    @pl.loop(0, n // GROUP)
    def _(b):
        network(b, True, bk2_send, bk2_recv, s_bk2, r_bk2)

    gathered(g_t, fx, out_o, oblk)
    collect(bk2_send, bk2_recv, s_bk2, r_bk2)
    gathered(a_t, xr, out_a, ablk)

    def finish(k):
        q = ahead(k)
        copy_to(idx_send, idx_recv, s_idx, r_idx, q).wait_send()
        copy_to(blk_send, blk_recv, s_blk, r_blk, q).wait_send()
        copy_to(bk_send, bk_recv, s_bk, r_bk, q).wait_send()
        copy_to(fw_send, fw_recv, s_fw, r_fw, q).wait_send()
        copy_to(bk2_send, bk2_recv, s_bk2, r_bk2, q).wait_send()

    each(finish)


def local(
    band_n, lon_n,
    atm_state, ocean_state, wet_mask, remap_tiles, intersection_atm, intersection_ocean,
    intersection_tile, peer_count, w_in, w_mid, b_hidden, w_out, b_out, up_atm, up_ocean,
):
    n = band_n * lon_n
    ablk, ch, cells = atm_state.shape
    oblk = ocean_state.shape[0]
    cf = w_out.shape[0]
    slots = 2 * n
    live = (jnp.arange(2, dtype=jnp.int32)[:, None] < peer_count[0][None, :]).astype(jnp.int32)
    meta = jnp.concatenate([intersection_ocean[0].T, intersection_tile[0].T, live], axis=0).reshape(-1)
    b_cols = (b_hidden * 0.5).T
    vm = pl.BlockSpec(memory_space=pltpu.VMEM)
    sm = pl.BlockSpec(memory_space=pltpu.SMEM)

    def flux_buffer():
        return pltpu.VMEM((2, n, cf, cells), BF)

    out_a, out_o = pl.pallas_call(
        functools.partial(kernel, n, lon_n),
        out_shape=(
            jax.ShapeDtypeStruct((ablk * cf, cells), F32),
            jax.ShapeDtypeStruct((oblk * cf, cells), F32),
        ),
        in_specs=[sm] + [vm] * 13,
        out_specs=(vm, vm),
        scratch_shapes=[
            pltpu.VMEM((1, n, 1, 128), jnp.int32),
            pltpu.VMEM((1, n, 1, 128), jnp.int32),
            pltpu.SMEM((1, n, 1, 128), jnp.int32),
            pltpu.VMEM((2, n, ch, cells), BF),
            pltpu.VMEM((2, n, ch, cells), BF),
            flux_buffer(), flux_buffer(), flux_buffer(), flux_buffer(), flux_buffer(), flux_buffer(),
            pltpu.VMEM((w_in.shape[1], 2 * GROUP * cells), BF),
            pltpu.VMEM(w_in.shape, BF),
            pltpu.VMEM(w_mid.shape, BF),
            pltpu.VMEM((slots * cf, cells), F32),
            pltpu.VMEM((slots * cf, cells), F32),
            pltpu.VMEM((slots * cf, cells), F32),
            pltpu.VMEM((8, 128), F32),
            pltpu.VMEM((slots, slots), BF),
            pltpu.VMEM((ablk, slots), BF),
            pltpu.VMEM((slots, slots), BF),
            pltpu.VMEM((oblk, slots), BF),
            pltpu.SemaphoreType.DMA,
        ] + [pltpu.SemaphoreType.DMA((n,))] * 10,
        compiler_params=pltpu.CompilerParams(
            collective_id=0, has_side_effects=True, vmem_limit_bytes=60 * 1024 * 1024
        ),
    )(
        meta, intersection_atm, intersection_ocean, atm_state, ocean_state, wet_mask, remap_tiles,
        w_in, w_mid, b_cols, w_out, b_out[:, None], up_atm, up_ocean,
    )
    return out_a.reshape(ablk, cf, cells), out_o.reshape(oblk, cf, cells)


def solution(mesh):
    b3 = P(("band", "lon"), None, None)
    b2 = P(("band", "lon"), None)
    placed = (b3, b3, b2, P(), b3, b3, b3, b2) + (P(),) * 7
    return jax.shard_map(
        functools.partial(local, mesh.shape["band"], mesh.shape["lon"]),
        mesh=mesh,
        in_specs=placed,
        out_specs=(b3, b3),
        check_vma=False,
    )
```
